32 devices in a mesh: freq: 4 (over z), bl: 8 (over y, x, core).
Axes of the slice: x: 2, y: 2, z: 4, core: 2. Of those that a mesh axis runs over, the one named last changes fastest.
Arguments:
- vis: float32 [2, 128, 16384], P(None, 'freq', 'bl'), may hold values from -60 to 60
- coherency: bfloat16 [2, 4, 128, 16384], P(None, None, 'freq', 'bl'), may hold values from -6 to 6
- gains_init: float32 [2, 4, 128, 512], P(None, None, 'freq', 'bl'), may hold values from -4 to 4
- station_pairs: int32 [2, 16384], P(None, 'bl'), may hold values from 0 to 511, as said below
Outputs:
- gains: float32 [2, 4, 128, 512], P(None, None, 'freq', 'bl')
- consensus: float32 [2, 4, 128, 512], P(None, None, 'freq', 'bl')
The draws below stay inside these ranges and needn't reach their ends.
Inputs may be any that keep to these rules, and one draw needn't show every extreme that they name: `station_pairs`: in each column the two stations differ.
All inputs are finite; a program needn't handle non-finite values.
Results may differ from the reference program's by a relative error of at most 0.0013.
Values may be sent and summed in bfloat16 or wider, within the bound.
A program may use at most 64 MiB of HBM per device.

```python
import math
import jax
import jax.numpy as jnp
from jax import lax

STATION_TOTAL = 512
SKY_DIRECTIONS = 4
CHANNELS_LOCAL = 32
ITERS = 2
ROUNDS = 2
CHANNEL_TOTAL = 128
BASELINE_TOTAL = 16384


def pair_draw(key):
    folded_key = jax.random.fold_in(key, 101)
    first_station_key, offset_key = jax.random.split(folded_key)
    first_station = jax.random.randint(first_station_key, (BASELINE_TOTAL,), 0, STATION_TOTAL, dtype=jnp.int32)
    offset_sample = jax.random.randint(offset_key, (BASELINE_TOTAL,), 1, STATION_TOTAL, dtype=jnp.int32)
    second = (first_station + offset_sample) % STATION_TOTAL
    first_station = first_station.at[0].set(0)
    second = second.at[0].set(STATION_TOTAL - 1)
    return jnp.stack([first_station, second]).astype(jnp.int32)


def coherency_draw(key):
    folded_key = jax.random.fold_in(key, 102)
    value_rows = jax.random.normal(folded_key, (2, SKY_DIRECTIONS, CHANNEL_TOTAL, BASELINE_TOTAL), dtype=jnp.float32)
    return jnp.clip(value_rows, -6.0, 6.0)


def draw_station_pairs(key, part):
    return pair_draw(key)


def draw_coherency(key, part):
    return coherency_draw(key).astype(jnp.bfloat16)


def draw_vis(key, part):
    pairs = pair_draw(key)
    coh = coherency_draw(key).astype(jnp.bfloat16).astype(jnp.float32)
    folded_key = jax.random.fold_in(key, 103)
    key_amp, key_phase, key_wobble, noise_key = jax.random.split(folded_key, 4)
    amplitude = 1.0 + 0.2 * jnp.clip(jax.random.normal(key_amp, (SKY_DIRECTIONS, CHANNEL_TOTAL, STATION_TOTAL), dtype=jnp.float32), -3.0, 3.0)
    phase = jax.random.uniform(key_phase, (SKY_DIRECTIONS, 1, STATION_TOTAL), minval=-math.pi, maxval=math.pi, dtype=jnp.float32)
    phase = phase + 0.3 * jnp.clip(jax.random.normal(key_wobble, (SKY_DIRECTIONS, CHANNEL_TOTAL, STATION_TOTAL), dtype=jnp.float32), -3.0, 3.0)
    true_re = amplitude * jnp.cos(phase)
    true_im = amplitude * jnp.sin(phase)
    near_re = jnp.take(true_re, pairs[0], axis=2)
    near_im = jnp.take(true_im, pairs[0], axis=2)
    far_re = jnp.take(true_re, pairs[1], axis=2)
    far_im = jnp.take(true_im, pairs[1], axis=2)
    z_re = coh[0] * far_re + coh[1] * far_im
    z_im = coh[1] * far_re - coh[0] * far_im
    model_re = jnp.sum(near_re * z_re - near_im * z_im, axis=0)
    model_im = jnp.sum(near_re * z_im + near_im * z_re, axis=0)
    noise_sample = 0.3 * jnp.clip(jax.random.normal(noise_key, (2, CHANNEL_TOTAL, BASELINE_TOTAL), dtype=jnp.float32), -4.0, 4.0)
    return jnp.clip(jnp.stack([model_re, model_im]) + noise_sample, -60.0, 60.0)


def steps_of(own_key, dims, pieces, smallest, top_value):
    def one(dim, shards_of):
        steps = jax.random.uniform(jax.random.fold_in(jax.random.fold_in(own_key, 6), dim), (shards_of,), jnp.float32, smallest / len(pieces), top_value / len(pieces))
        return jnp.repeat(jnp.exp(steps), dims[dim] // shards_of).reshape((-1,) + (1,) * (len(dims) - dim - 1))

    loudness = one(*pieces[0])
    for cut in pieces[1:]:
        loudness = loudness * one(*cut)
    return loudness


def scatter_about(rng, extent, width, limit, shards=(), held_as=jnp.bfloat16):
    entries = jax.random.normal(rng, extent, jnp.float32) * width
    if len(shards) > 0:
        entries = steps_of(rng, extent, shards, -0.22, 0.18) * entries
    return jnp.clip(entries, min=-limit, max=limit).astype(held_as)


def setup_inputs(seed: int = 0) -> dict:
    splits = jax.random.split(jax.random.key(seed), 5)
    vis = draw_vis(jax.random.fold_in(splits[4], 71), 0)
    coherency = draw_coherency(jax.random.fold_in(splits[4], 71), 0)
    gains_init = scatter_about(splits[2], (2, SKY_DIRECTIONS, CHANNEL_TOTAL, STATION_TOTAL), 0.7, 4.0, ((2, 4), (3, 8)), jnp.float32)
    station_pairs = draw_station_pairs(jax.random.fold_in(splits[4], 71), 0)
    return {"vis": vis, "coherency": coherency, "gains_init": gains_init, "station_pairs": station_pairs}


def basis_rows(channels):
    position = (2.0 * jnp.arange(channels, dtype=jnp.float32) + 1.0) / channels - 1.0
    raw = [jnp.ones_like(position), position, position * position, position * position * position]
    rows = []
    for vector in raw:
        for other in rows:
            vector = vector - jnp.sum(other * vector) * other
        rows.append(vector / jnp.sqrt(jnp.sum(vector * vector)))
    return jnp.stack(rows)

def model_terms(vis, coherency, near, far):
    coh_re = coherency[0].astype(jnp.float32)
    coh_im = coherency[1].astype(jnp.float32)
    z_re = coh_re * far[0] + coh_im * far[1]
    z_im = coh_im * far[0] - coh_re * far[1]
    x_re = near[0] * coh_re - near[1] * coh_im
    x_im = near[0] * coh_im + near[1] * coh_re
    model_re = lax.optimization_barrier(jnp.sum(near[0] * z_re - near[1] * z_im, axis=0))
    model_im = lax.optimization_barrier(jnp.sum(near[0] * z_im + near[1] * z_re, axis=0))
    res_re = (vis[0] - model_re)[None]
    res_im = (vis[1] - model_im)[None]
    first_terms = jnp.stack([res_re * z_re + res_im * z_im, res_im * z_re - res_re * z_im, z_re * z_re + z_im * z_im]).astype(jnp.bfloat16)
    second_terms = jnp.stack([res_re * x_re + res_im * x_im, res_re * x_im - res_im * x_re, x_re * x_re + x_im * x_im]).astype(jnp.bfloat16)
    return (first_terms, second_terms)

def advance(gains, sums, target, penalty_weight):
    return gains + (sums[0:2] + penalty_weight * (target - gains)) / (2.0 * sums[2] + penalty_weight)

def station_total(terms, index):
    moved = jnp.moveaxis(terms.astype(jnp.float32), 3, 0)
    summed = jax.ops.segment_sum(moved, index, num_segments=STATION_TOTAL)
    return jnp.moveaxis(summed, 0, 3)

def reference(vis, coherency, gains_init, station_pairs):
    basis = basis_rows(CHANNEL_TOTAL)
    penalty_weight = 2.0 * BASELINE_TOTAL / STATION_TOTAL
    first_index = station_pairs[0]
    second_index = station_pairs[1]
    block_list = CHANNEL_TOTAL // CHANNELS_LOCAL
    visibility_blocks = jnp.moveaxis(vis.reshape(2, block_list, CHANNELS_LOCAL, BASELINE_TOTAL), 1, 0)
    coherency_blocks = jnp.moveaxis(coherency.reshape(2, SKY_DIRECTIONS, block_list, CHANNELS_LOCAL, BASELINE_TOTAL), 2, 0)

    def one_block(items):
        vis_part, coh_part, gain_part, target_part = items
        rounded = lax.optimization_barrier(gain_part.astype(jnp.bfloat16)).astype(jnp.float32)
        near = jnp.take(rounded, first_index, axis=3)
        far = jnp.take(rounded, second_index, axis=3)
        first_terms, second_terms = model_terms(vis_part, coh_part, near, far)
        sums = station_total(first_terms, first_index) + station_total(second_terms, second_index)
        return advance(gain_part, sums, target_part, penalty_weight)

    def sweep(gains, target):
        gain_blocks = jnp.moveaxis(gains.reshape(2, SKY_DIRECTIONS, block_list, CHANNELS_LOCAL, STATION_TOTAL), 2, 0)
        target_blocks = jnp.moveaxis(target.reshape(2, SKY_DIRECTIONS, block_list, CHANNELS_LOCAL, STATION_TOTAL), 2, 0)
        result = lax.map(one_block, (visibility_blocks, coherency_blocks, gain_blocks, target_blocks))
        return jnp.moveaxis(result, 0, 2).reshape(2, SKY_DIRECTIONS, CHANNEL_TOTAL, STATION_TOTAL)
    gains = gains_init
    target = gains_init
    dual = jnp.zeros_like(gains_init)
    consensus = gains_init
    for round_index in range(ROUNDS):
        for step_index in range(ITERS):
            gains = sweep(gains, target)
        blend = gains + dual
        coefficients = jnp.einsum('jk,adks->jads', basis, blend, precision=lax.Precision.HIGHEST)
        consensus = jnp.einsum('jk,jads->adks', basis, coefficients, precision=lax.Precision.HIGHEST)
        dual = dual + gains - consensus
        target = consensus - dual
    return (gains, consensus)
```

```python
import functools

import numpy as np
import jax
import jax.numpy as jnp
from jax import lax
from jax.experimental import pallas as pl
from jax.experimental.pallas import tpu as pltpu
from jax.sharding import PartitionSpec as P

STATION_TOTAL = 512
SKY_DIRECTIONS = 4
ITERS = 2
ROUNDS = 2
JD = 4
MESH = pl.DeviceIdType.MESH
HIGH = lax.Precision.HIGHEST
F32 = jnp.float32
BF16 = jnp.bfloat16
LO = 128
VMEM_CAP = 60 * 1024 * 1024


def basis_rows(channels):
    position = (2.0 * np.arange(channels, dtype=np.float32) + np.float32(1.0)) / np.float32(channels) - np.float32(1.0)
    raw = [np.ones_like(position), position, position * position, position * position * position]
    rows = []
    for vector in raw:
        for other in rows:
            vector = vector - np.sum(other * vector, dtype=np.float32) * other
        rows.append(vector / np.sqrt(np.sum(vector * vector, dtype=np.float32)))
    return np.stack(rows).astype(np.float32)


def greet(axes):
    barrier = pltpu.get_barrier_semaphore()
    count = 0
    for axis in axes:
        n = lax.axis_size(axis)
        me = lax.axis_index(axis)
        for o in range(1, n):
            pl.semaphore_signal(barrier, inc=1, device_id={axis: lax.rem(me + o, n)}, device_id_type=MESH)
            count += 1
    pl.semaphore_wait(barrier, count)


def sum_directions(x, cl):
    rows = x.shape[0]
    dirs = rows // cl
    if cl == 4 and rows == 16:
        half = x[:8] + x[8:]
        half = half + pltpu.roll(half, 4, 0)
        return jnp.concatenate([half, half], axis=0)
    total = x[:cl]
    for d in range(1, dirs):
        total = total + x[d * cl : (d + 1) * cl]
    return jnp.concatenate([total] * dirs, axis=0)


def flip(me, o, n):
    value = 0
    bit = 1
    while bit < n:
        value = value + lax.rem(lax.rem(lax.div(me, bit), 2) + lax.rem(lax.div(o, bit), 2), 2) * bit
        bit *= 2
    return value


def calibrate_kernel(
    n, m, cl, rho,
    coh_in, vis_in, gains_in, pairs_in, wide_ref, basis_ref,
    gains_ref, cons_ref,
    coh_all, vis_all, gains_all, pairs_all, onehot, table, acc,
    part, got, chunk, got_f, whole, coef, fit_out, gains_send, got_b, got_g, chunk_b, got_fb,
    sx, rx, lx, s1, r1, s2, r2, s3, r3, s4, r4, s5, r5,
):
    dirs = SKY_DIRECTIONS
    rows = dirs * cl
    lo = LO
    hi = STATION_TOTAL // lo
    per = vis_in.shape[2]
    owned = STATION_TOTAL // n
    me = lax.axis_index("bl")
    me_f = lax.axis_index("freq")
    greet(("bl", "freq"))

    def transfer(a, o, peer, src, slot):
        ref = (gains_in, pairs_in, coh_in, vis_in)[a]
        dst = (gains_all, pairs_all, coh_all, vis_all)[a]
        return pltpu.make_async_remote_copy(
            ref if a == 1 else ref.at[src], dst.at[slot], sx.at[a, o - 1], rx.at[a, o - 1],
            device_id={"bl": peer}, device_id_type=MESH,
        )

    sends = []
    for group in ((0, 1), (2, 3)):
        for o in range(1, n):
            peer = flip(me, o, n)
            for a in group:
                copy = transfer(a, o, peer, peer, me)
                copy.start()
                sends.append(copy)
    own = [
        pltpu.make_async_copy(gains_in.at[me], gains_all.at[me], lx.at[0]),
        pltpu.make_async_copy(pairs_in, pairs_all.at[me], lx.at[1]),
        pltpu.make_async_copy(coh_in.at[me], coh_all.at[me], lx.at[2]),
        pltpu.make_async_copy(vis_in.at[me], vis_all.at[me], lx.at[3]),
    ]
    for copy in own:
        copy.start()
    for copy in own:
        copy.wait()
    for o in range(1, n):
        transfer(0, o, flip(me, o, n), me, flip(me, o, n)).wait_recv()

    wide = wide_ref[me_f * n + me]

    def build(block):
        station = lax.broadcasted_iota(jnp.int32, (lo, per), 0)
        for t in range(2):
            index = pairs_all[block, t : t + 1, :] & (lo - 1)
            onehot[t, block] = jnp.where(station == index, 1.0, 0.0).astype(BF16)

    def pick(x, group):
        value = x[: 2 * rows]
        for h in range(1, hi):
            value = jnp.where(group == h, x[2 * rows * h : 2 * rows * (h + 1)], value)
        return value

    def spread(terms, group):
        terms = jnp.concatenate(terms, axis=0).astype(BF16)
        return jnp.concatenate(
            [
                terms * jnp.broadcast_to(jnp.where(group == h, 1.0, 0.0), (3 * rows, per)).astype(BF16)
                for h in range(hi)
            ],
            axis=0,
        )

    def add_block(block):
        group0 = lax.shift_right_logical(pairs_all[block, 0:1, :], lo.bit_length() - 1)
        group1 = lax.shift_right_logical(pairs_all[block, 1:2, :], lo.bit_length() - 1)
        ohn = onehot[0, block]
        ohf = onehot[1, block]
        near = pick(jnp.dot(table[...], ohn, preferred_element_type=F32), group0)
        far = pick(jnp.dot(table[...], ohf, preferred_element_type=F32), group1)
        nr, ni = near[:rows], near[rows:]
        fr, fi = far[:rows], far[rows:]
        cr = coh_all[block, 0].astype(F32)
        ci = coh_all[block, 1].astype(F32)
        zr = cr * fr + ci * fi
        zi = ci * fr - cr * fi
        xr = nr * cr - ni * ci
        xi = nr * ci + ni * cr
        mr = sum_directions(nr * zr - ni * zi, cl)
        mi = sum_directions(nr * zi + ni * zr, cl)
        v = vis_all[block].astype(F32)
        rr = jnp.concatenate([v[:cl]] * dirs, axis=0) - mr
        ri = jnp.concatenate([v[cl:]] * dirs, axis=0) - mi
        t1 = spread([rr * zr + ri * zi, ri * zr - rr * zi, zr * zr + zi * zi], group0)
        t2 = spread([rr * xr + ri * xi, rr * xi - ri * xr, xr * xr + xi * xi], group1)
        contract = (((1,), (1,)), ((), ()))
        acc[...] += lax.dot_general(t1, ohn, contract, preferred_element_type=F32) + lax.dot_general(
            t2, ohf, contract, preferred_element_type=F32
        )

    def load_table(gains):
        rounded = gains.astype(BF16)
        table[...] = jnp.concatenate([rounded[:, h * lo : (h + 1) * lo] for h in range(hi)], axis=0)
        acc[...] = jnp.zeros_like(acc)

    def advance(gains, target):
        sums = jnp.concatenate([acc[3 * rows * h : 3 * rows * (h + 1)] for h in range(hi)], axis=1)
        below = 2.0 * sums[2 * rows :] + rho
        below = jnp.concatenate([below, below], axis=0)
        return gains + (sums[: 2 * rows] + rho * (target - gains)) / below

    def again(block, carry):
        add_block(block)
        return carry

    def whole_rows(ref):
        blocks = [ref[s] for s in range(n)]
        return jnp.concatenate(
            [jnp.concatenate([b[:, a * owned : (a + 1) * owned] for b in blocks], axis=1) for a in range(2)], axis=0
        )

    def block_of(x, s):
        half = x.shape[0] // 2
        return jnp.concatenate([x[:half, s * owned : (s + 1) * owned], x[half:, s * owned : (s + 1) * owned]], axis=1)

    def start_freq(src, slots, send, recv):
        copies = []
        for o in range(1, m):
            copy = pltpu.make_async_remote_copy(
                src, slots.at[o - 1], send.at[o - 1], recv.at[o - 1],
                device_id={"freq": lax.rem(me_f + o, m)}, device_id_type=MESH,
            )
            copy.start()
            copies.append(copy)
        return copies

    def sum_freq(copies, total, slots):
        for o in range(1, m):
            copies[o - 1].wait()
            total = total + slots[o - 1]
        return total

    gains = whole_rows(gains_all)
    target = gains
    load_table(gains)

    def arriving(o, carry):
        peer = flip(me, o, n)
        for a in (1, 2, 3):
            transfer(a, o, peer, me, peer).wait_recv()
        build(peer)
        add_block(peer)
        return carry

    build(me)
    add_block(me)
    lax.fori_loop(1, n, arriving, 0)
    gains = advance(gains, target)
    for _ in range(ITERS - 1):
        load_table(gains)
        lax.fori_loop(0, n, again, 0)
        gains = advance(gains, target)
    for copy in sends:
        copy.wait_send()

    fitted = jnp.dot(wide, gains, precision=HIGH, preferred_element_type=F32)
    for s in range(n):
        part[s] = block_of(fitted, s)
    copies = []
    for o in range(1, n):
        peer = flip(me, o, n)
        copy = pltpu.make_async_remote_copy(
            part.at[peer], got.at[o - 1], s1.at[o - 1], r1.at[o - 1],
            device_id={"bl": peer}, device_id_type=MESH,
        )
        copy.start()
        copies.append(copy)
    load_table(gains)
    cut = (n * 3 // 8, n * 6 // 8)
    lax.fori_loop(0, cut[0], again, 0)
    total = part[me]
    for o in range(1, n):
        copies[o - 1].wait()
        total = total + got[o - 1]
    chunk[...] = total
    copies = start_freq(chunk, got_f, s2, r2)
    lax.fori_loop(cut[0], cut[1], again, 0)
    total = sum_freq(copies, total, got_f)
    whole[...] = total
    copies = []
    for o in range(1, n):
        copy = pltpu.make_async_remote_copy(
            whole, coef.at[me], s3.at[o - 1], r3.at[o - 1],
            device_id={"bl": flip(me, o, n)}, device_id_type=MESH,
        )
        copy.start()
        copies.append(copy)
    coef[me] = total
    lax.fori_loop(cut[1], n, again, 0)
    for copy in copies:
        copy.wait_send()
    for o in range(1, n):
        peer = flip(me, o, n)
        pltpu.make_async_remote_copy(
            whole, coef.at[peer], s3.at[o - 1], r3.at[o - 1],
            device_id={"bl": peer}, device_id_type=MESH,
        ).wait_recv()

    consensus = lax.dot_general(
        wide, whole_rows(coef), (((0,), (0,)), ((), ())), precision=HIGH, preferred_element_type=F32
    )
    dual = gains - consensus
    target = consensus - dual
    gains = advance(gains, target)
    for _ in range(ITERS - 1):
        load_table(gains)
        lax.fori_loop(0, n, again, 0)
        gains = advance(gains, target)

    fitted = jnp.dot(wide, gains + dual, precision=HIGH, preferred_element_type=F32)
    for s in range(n):
        fit_out[s] = block_of(fitted, s)
        gains_send[s] = block_of(gains, s)

    def deliver(k, o, peer, slot):
        src, dst = ((fit_out, got_b), (gains_send, got_g))[k]
        return pltpu.make_async_remote_copy(
            src.at[peer], dst.at[slot], s4.at[k, o - 1], r4.at[k, o - 1],
            device_id={"bl": peer}, device_id_type=MESH,
        )

    copies = []
    for k in range(2):
        for o in range(1, n):
            copy = deliver(k, o, flip(me, o, n), me)
            copy.start()
            copies.append(copy)
    got_b[me] = fit_out[me]
    got_g[me] = gains_send[me]
    for o in range(1, n):
        deliver(0, o, flip(me, o, n), flip(me, o, n)).wait_recv()
    total = got_b[0]
    for s in range(1, n):
        total = total + got_b[s]
    chunk_b[...] = total
    total = sum_freq(start_freq(chunk_b, got_fb, s5, r5), total, got_fb)
    for o in range(1, n):
        deliver(1, o, flip(me, o, n), flip(me, o, n)).wait_recv()
    for copy in copies:
        copy.wait_send()
    for s in range(n):
        for a in range(2):
            for d in range(dirs):
                gains_ref[a, d, s * cl : (s + 1) * cl, :] = got_g[s, d * cl : (d + 1) * cl, a * owned : (a + 1) * owned]
    mine = basis_ref[me_f]
    for a in range(2):
        for d in range(dirs):
            value = None
            for j in range(JD):
                row = j * dirs + d
                term = mine[:, j : j + 1] * total[row : row + 1, a * owned : (a + 1) * owned]
                value = term if value is None else value + term
            cons_ref[a, d] = value


def calibrate(n, m, cl, rho, args, shape):
    coh, vis, gains, pairs = args[:4]
    rows = SKY_DIRECTIONS * cl
    hi = STATION_TOTAL // LO
    per = vis.shape[2]
    owned = STATION_TOTAL // n
    chunk = (JD * SKY_DIRECTIONS, 2 * owned)
    dma = pltpu.SemaphoreType.DMA
    vm = pltpu.VMEM
    return pl.pallas_call(
        functools.partial(calibrate_kernel, n, m, cl, rho),
        out_shape=[jax.ShapeDtypeStruct(shape, F32)] * 2,
        in_specs=[pl.BlockSpec(memory_space=pltpu.VMEM)] * len(args),
        out_specs=[pl.BlockSpec(memory_space=pltpu.VMEM)] * 2,
        scratch_shapes=[
            vm(coh.shape, coh.dtype), vm(vis.shape, vis.dtype), vm(gains.shape, F32), vm((n,) + pairs.shape, jnp.int32),
            vm((2, n, LO, per), BF16), vm((hi * 2 * rows, LO), BF16), vm((hi * 3 * rows, LO), F32),
            vm((n,) + chunk, F32), vm((n - 1,) + chunk, F32), vm(chunk, F32),
            vm((m - 1,) + chunk, F32), vm(chunk, F32), vm((n,) + chunk, F32),
            vm((n,) + chunk, F32), vm(gains.shape, F32), vm((n,) + chunk, F32), vm(gains.shape, F32),
            vm(chunk, F32), vm((m - 1,) + chunk, F32),
            dma((4, n - 1)), dma((4, n - 1)), dma((4,)),
            dma((n - 1,)), dma((n - 1,)), dma((m - 1,)), dma((m - 1,)), dma((n - 1,)), dma((n - 1,)),
            dma((2, n - 1)), dma((2, n - 1)), dma((m - 1,)), dma((m - 1,)),
        ],
        compiler_params=pltpu.CompilerParams(collective_id=0, has_side_effects=True, vmem_limit_bytes=VMEM_CAP),
    )(*args)


def shards(n, m, vis, coherency, gains_init, station_pairs):
    dirs = SKY_DIRECTIONS
    channels = vis.shape[1]
    per = vis.shape[2]
    owned = gains_init.shape[3]
    cl = channels // n
    rows = dirs * cl
    rho = 2.0 * per * n / STATION_TOTAL
    basis = basis_rows(channels * m)
    wide = np.zeros((m * n, 2, JD, dirs, 2, dirs, cl), np.float32)
    split = basis.reshape(JD, m * n, cl)
    for a in range(2):
        for d in range(dirs):
            wide[:, a, :, d, a, d, :] = np.moveaxis(split, 1, 0)
    wide = jnp.asarray(wide.reshape(m * n, JD * 2 * dirs, 2 * rows))
    basis_t = jnp.asarray(np.ascontiguousarray(basis.reshape(JD, m, channels).transpose(1, 2, 0)))

    coh_out = coherency.reshape(2, dirs, n, cl, per).transpose(2, 0, 1, 3, 4).reshape(n, 2, rows, per)
    vis_out = vis.reshape(2, n, cl, per).transpose(1, 0, 2, 3).reshape(n, 2 * cl, per).astype(BF16)
    gains_out = gains_init.reshape(2, dirs, n, cl, owned).transpose(2, 1, 3, 0, 4).reshape(n, rows, 2 * owned)
    args = (coh_out, vis_out, gains_out, station_pairs, wide, basis_t)
    return tuple(calibrate(n, m, cl, rho, args, gains_init.shape))


def solution(mesh):
    placed = (
        P(None, "freq", "bl"),
        P(None, None, "freq", "bl"),
        P(None, None, "freq", "bl"),
        P(None, "bl"),
    )
    return jax.shard_map(
        functools.partial(shards, mesh.shape["bl"], mesh.shape["freq"]),
        mesh=mesh,
        in_specs=placed,
        out_specs=(P(None, None, "freq", "bl"), P(None, None, "freq", "bl")),
        check_vma=False,
    )
```

```python
import functools

import numpy as np
import jax
import jax.numpy as jnp
from jax import lax
from jax.experimental import pallas as pl
from jax.experimental.pallas import tpu as pltpu
from jax.sharding import PartitionSpec as P

STATION_TOTAL = 512
SKY_DIRECTIONS = 4
ITERS = 2
ROUNDS = 2
JD = 4
MESH = pl.DeviceIdType.MESH
HIGH = lax.Precision.HIGHEST
F32 = jnp.float32
BF16 = jnp.bfloat16
LO = 128
VIS_TOP = 60.0
VIS_STEPS = 32767.0
VMEM_CAP = 60 * 1024 * 1024


def basis_rows(channels):
    position = (2.0 * np.arange(channels, dtype=np.float32) + np.float32(1.0)) / np.float32(channels) - np.float32(1.0)
    raw = [np.ones_like(position), position, position * position, position * position * position]
    rows = []
    for vector in raw:
        for other in rows:
            vector = vector - np.sum(other * vector, dtype=np.float32) * other
        rows.append(vector / np.sqrt(np.sum(vector * vector, dtype=np.float32)))
    return np.stack(rows).astype(np.float32)


def greet(axes):
    barrier = pltpu.get_barrier_semaphore()
    for axis in axes:
        n = lax.axis_size(axis)
        me = lax.axis_index(axis)
        for o in range(1, n):
            pl.semaphore_signal(barrier, inc=1, device_id={axis: lax.rem(me + o, n)}, device_id_type=MESH)


def meet(axes):
    count = sum(lax.axis_size(axis) - 1 for axis in axes)
    pl.semaphore_wait(pltpu.get_barrier_semaphore(), count)


def sum_directions(x, cl):
    rows = x.shape[0]
    dirs = rows // cl
    if cl == 4 and rows == 16:
        half = x[:8] + x[8:]
        half = half + pltpu.roll(half, 4, 0)
        return jnp.concatenate([half, half], axis=0)
    total = x[:cl]
    for d in range(1, dirs):
        total = total + x[d * cl : (d + 1) * cl]
    return jnp.concatenate([total] * dirs, axis=0)


def flip(me, o, n):
    value = 0
    bit = 1
    while bit < n:
        value = value + lax.rem(lax.rem(lax.div(me, bit), 2) + lax.rem(lax.div(o, bit), 2), 2) * bit
        bit *= 2
    return value


def calibrate_kernel(
    n, m, cl, rho,
    coh_raw, vis_raw, gains_raw, pairs_in, wide_raw, basis_raw,
    gains_ref, cons_ref,
    coh_own, vis_own, gains_own, wide_ref, basis_ref, coh_send, vis_send,
    coh_all, vis_all, gains_all, pairs_all, onehot, table, acc,
    part, got, chunk, got_f, whole, coef, fit_out, gains_send, got_b, got_g, chunk_b, got_fb,
    lr, sx, rx, lx, s1, r1, s2, r2, s3, r3, s4, r4, s5, r5,
):
    dirs = SKY_DIRECTIONS
    rows = dirs * cl
    lo = LO
    hi = STATION_TOTAL // lo
    per = vis_raw.shape[2]
    owned = STATION_TOTAL // n
    me = lax.axis_index("bl")
    me_f = lax.axis_index("freq")
    greet(("bl", "freq"))
    loads = [
        pltpu.make_async_copy(gains_raw, gains_own, lr.at[0]),
        pltpu.make_async_copy(coh_raw, coh_own, lr.at[1]),
        pltpu.make_async_copy(vis_raw, vis_own, lr.at[2]),
        pltpu.make_async_copy(wide_raw.at[me_f * n + me], wide_ref, lr.at[3]),
        pltpu.make_async_copy(basis_raw.at[me_f], basis_ref, lr.at[4]),
    ]
    for copy in loads:
        copy.start()

    def transfer(a, o, peer, src, slot):
        ref = (gains_send, pairs_in, coh_send, vis_send)[a]
        dst = (gains_all, pairs_all, coh_all, vis_all)[a]
        return pltpu.make_async_remote_copy(
            ref if a == 1 else ref.at[src], dst.at[slot], sx.at[a, o - 1], rx.at[a, o - 1],
            device_id={"bl": peer}, device_id_type=MESH,
        )

    def of(x, s):
        return x[s * cl : (s + 1) * cl]

    loads[0].wait()
    parts = [[gains_own[a, d] for d in range(dirs)] for a in range(2)]
    for s in range(n):
        gains_send[s] = jnp.concatenate(
            [jnp.concatenate([of(x, s) for x in parts[a]], axis=0) for a in range(2)], axis=1
        )
    loads[1].wait()
    for a in range(2):
        parts = [coh_own[a, d].astype(F32) for d in range(dirs)]
        for s in range(n):
            coh_send[s, a] = jnp.concatenate([of(x, s) for x in parts], axis=0).astype(BF16)
    loads[2].wait()
    parts = [jnp.round(vis_own[a] * (VIS_STEPS / VIS_TOP)).astype(jnp.int32) for a in range(2)]
    for s in range(n):
        vis_send[s] = jnp.concatenate([of(x, s) for x in parts], axis=0).astype(jnp.int16)
    for copy in loads[3:]:
        copy.wait()
    meet(("bl", "freq"))

    sends = []
    for group in ((0, 1), (2, 3)):
        for o in range(1, n):
            peer = flip(me, o, n)
            for a in group:
                copy = transfer(a, o, peer, peer, me)
                copy.start()
                sends.append(copy)
    own = [
        pltpu.make_async_copy(gains_send.at[me], gains_all.at[me], lx.at[0]),
        pltpu.make_async_copy(pairs_in, pairs_all.at[me], lx.at[1]),
        pltpu.make_async_copy(coh_send.at[me], coh_all.at[me], lx.at[2]),
        pltpu.make_async_copy(vis_send.at[me], vis_all.at[me], lx.at[3]),
    ]
    for copy in own:
        copy.start()
    for copy in own:
        copy.wait()
    for o in range(1, n):
        transfer(0, o, flip(me, o, n), me, flip(me, o, n)).wait_recv()

    wide = wide_ref[...]

    def build(block):
        station = lax.broadcasted_iota(jnp.int32, (lo, per), 0)
        for t in range(2):
            index = pairs_all[block, t : t + 1, :] & (lo - 1)
            onehot[t, block] = jnp.where(station == index, 1.0, 0.0).astype(BF16)

    def pick(x, group):
        value = x[: 2 * rows]
        for h in range(1, hi):
            value = jnp.where(group == h, x[2 * rows * h : 2 * rows * (h + 1)], value)
        return value

    def spread(terms, group):
        terms = jnp.concatenate(terms, axis=0).astype(BF16)
        return jnp.concatenate(
            [
                terms * jnp.broadcast_to(jnp.where(group == h, 1.0, 0.0), (3 * rows, per)).astype(BF16)
                for h in range(hi)
            ],
            axis=0,
        )

    def add_block(block):
        group0 = lax.shift_right_logical(pairs_all[block, 0:1, :], lo.bit_length() - 1)
        group1 = lax.shift_right_logical(pairs_all[block, 1:2, :], lo.bit_length() - 1)
        ohn = onehot[0, block]
        ohf = onehot[1, block]
        near = pick(jnp.dot(table[...], ohn, preferred_element_type=F32), group0)
        far = pick(jnp.dot(table[...], ohf, preferred_element_type=F32), group1)
        nr, ni = near[:rows], near[rows:]
        fr, fi = far[:rows], far[rows:]
        cr = coh_all[block, 0].astype(F32)
        ci = coh_all[block, 1].astype(F32)
        zr = cr * fr + ci * fi
        zi = ci * fr - cr * fi
        xr = nr * cr - ni * ci
        xi = nr * ci + ni * cr
        mr = sum_directions(nr * zr - ni * zi, cl)
        mi = sum_directions(nr * zi + ni * zr, cl)
        v = vis_all[block].astype(jnp.int32).astype(F32) * (VIS_TOP / VIS_STEPS)
        rr = jnp.concatenate([v[:cl]] * dirs, axis=0) - mr
        ri = jnp.concatenate([v[cl:]] * dirs, axis=0) - mi
        t1 = spread([rr * zr + ri * zi, ri * zr - rr * zi, zr * zr + zi * zi], group0)
        t2 = spread([rr * xr + ri * xi, rr * xi - ri * xr, xr * xr + xi * xi], group1)
        contract = (((1,), (1,)), ((), ()))
        acc[...] += lax.dot_general(t1, ohn, contract, preferred_element_type=F32) + lax.dot_general(
            t2, ohf, contract, preferred_element_type=F32
        )

    def load_table(gains):
        rounded = gains.astype(BF16)
        table[...] = jnp.concatenate([rounded[:, h * lo : (h + 1) * lo] for h in range(hi)], axis=0)
        acc[...] = jnp.zeros_like(acc)

    def advance(gains, target):
        sums = jnp.concatenate([acc[3 * rows * h : 3 * rows * (h + 1)] for h in range(hi)], axis=1)
        below = 2.0 * sums[2 * rows :] + rho
        below = jnp.concatenate([below, below], axis=0)
        return gains + (sums[: 2 * rows] + rho * (target - gains)) / below

    def again(block, carry):
        add_block(block)
        return carry

    def whole_rows(ref):
        blocks = [ref[s] for s in range(n)]
        return jnp.concatenate(
            [jnp.concatenate([b[:, a * owned : (a + 1) * owned] for b in blocks], axis=1) for a in range(2)], axis=0
        )

    def block_of(x, s):
        half = x.shape[0] // 2
        return jnp.concatenate([x[:half, s * owned : (s + 1) * owned], x[half:, s * owned : (s + 1) * owned]], axis=1)

    def start_freq(src, slots, send, recv):
        copies = []
        for o in range(1, m):
            copy = pltpu.make_async_remote_copy(
                src, slots.at[o - 1], send.at[o - 1], recv.at[o - 1],
                device_id={"freq": lax.rem(me_f + o, m)}, device_id_type=MESH,
            )
            copy.start()
            copies.append(copy)
        return copies

    def sum_freq(copies, total, slots):
        for o in range(1, m):
            copies[o - 1].wait()
            total = total + slots[o - 1]
        return total

    gains = whole_rows(gains_all)
    target = gains
    load_table(gains)

    def arriving(o, carry):
        peer = flip(me, o, n)
        for a in (1, 2, 3):
            transfer(a, o, peer, me, peer).wait_recv()
        build(peer)
        add_block(peer)
        return carry

    build(me)
    add_block(me)
    lax.fori_loop(1, n, arriving, 0)
    gains = advance(gains, target)
    for _ in range(ITERS - 1):
        load_table(gains)
        lax.fori_loop(0, n, again, 0)
        gains = advance(gains, target)
    for copy in sends:
        copy.wait_send()

    fitted = jnp.dot(wide, gains, precision=HIGH, preferred_element_type=F32)
    for s in range(n):
        part[s] = block_of(fitted, s)
    copies = []
    for o in range(1, n):
        peer = flip(me, o, n)
        copy = pltpu.make_async_remote_copy(
            part.at[peer], got.at[o - 1], s1.at[o - 1], r1.at[o - 1],
            device_id={"bl": peer}, device_id_type=MESH,
        )
        copy.start()
        copies.append(copy)
    load_table(gains)
    cut = (n * 3 // 8, n * 6 // 8)
    lax.fori_loop(0, cut[0], again, 0)
    total = part[me]
    for o in range(1, n):
        copies[o - 1].wait()
        total = total + got[o - 1]
    chunk[...] = total
    copies = start_freq(chunk, got_f, s2, r2)
    lax.fori_loop(cut[0], cut[1], again, 0)
    total = sum_freq(copies, total, got_f)
    whole[...] = total
    copies = []
    for o in range(1, n):
        copy = pltpu.make_async_remote_copy(
            whole, coef.at[me], s3.at[o - 1], r3.at[o - 1],
            device_id={"bl": flip(me, o, n)}, device_id_type=MESH,
        )
        copy.start()
        copies.append(copy)
    coef[me] = total
    lax.fori_loop(cut[1], n, again, 0)
    for copy in copies:
        copy.wait_send()
    for o in range(1, n):
        peer = flip(me, o, n)
        pltpu.make_async_remote_copy(
            whole, coef.at[peer], s3.at[o - 1], r3.at[o - 1],
            device_id={"bl": peer}, device_id_type=MESH,
        ).wait_recv()

    consensus = lax.dot_general(
        wide, whole_rows(coef), (((0,), (0,)), ((), ())), precision=HIGH, preferred_element_type=F32
    )
    dual = gains - consensus
    target = consensus - dual
    gains = advance(gains, target)
    for _ in range(ITERS - 1):
        load_table(gains)
        lax.fori_loop(0, n, again, 0)
        gains = advance(gains, target)

    fitted = jnp.dot(wide, gains + dual, precision=HIGH, preferred_element_type=F32)
    for s in range(n):
        fit_out[s] = block_of(fitted, s)
        gains_send[s] = block_of(gains, s)

    def deliver(k, o, peer, slot):
        src, dst = ((fit_out, got_b), (gains_send, got_g))[k]
        return pltpu.make_async_remote_copy(
            src.at[peer], dst.at[slot], s4.at[k, o - 1], r4.at[k, o - 1],
            device_id={"bl": peer}, device_id_type=MESH,
        )

    copies = []
    for k in range(2):
        for o in range(1, n):
            copy = deliver(k, o, flip(me, o, n), me)
            copy.start()
            copies.append(copy)
    got_b[me] = fit_out[me]
    got_g[me] = gains_send[me]
    for o in range(1, n):
        deliver(0, o, flip(me, o, n), flip(me, o, n)).wait_recv()
    total = got_b[0]
    for s in range(1, n):
        total = total + got_b[s]
    chunk_b[...] = total
    total = sum_freq(start_freq(chunk_b, got_fb, s5, r5), total, got_fb)
    for o in range(1, n):
        deliver(1, o, flip(me, o, n), flip(me, o, n)).wait_recv()
    for copy in copies:
        copy.wait_send()
    for s in range(n):
        for a in range(2):
            for d in range(dirs):
                gains_ref[a, d, s * cl : (s + 1) * cl, :] = got_g[s, d * cl : (d + 1) * cl, a * owned : (a + 1) * owned]
    mine = basis_ref[...]
    for a in range(2):
        for d in range(dirs):
            value = None
            for j in range(JD):
                row = j * dirs + d
                term = mine[:, j : j + 1] * total[row : row + 1, a * owned : (a + 1) * owned]
                value = term if value is None else value + term
            cons_ref[a, d] = value


def calibrate(n, m, cl, rho, args, shape):
    coh, vis, gains, pairs, wide, basis = args
    rows = SKY_DIRECTIONS * cl
    hi = STATION_TOTAL // LO
    per = vis.shape[2]
    owned = STATION_TOTAL // n
    coh_split = (n, 2, rows, per)
    vis_split = (n, 2 * cl, per)
    gains_split = (n, rows, 2 * owned)
    chunk = (JD * SKY_DIRECTIONS, 2 * owned)
    dma = pltpu.SemaphoreType.DMA
    vm = pltpu.VMEM
    return pl.pallas_call(
        functools.partial(calibrate_kernel, n, m, cl, rho),
        out_shape=[jax.ShapeDtypeStruct(shape, F32)] * 2,
        in_specs=[pl.BlockSpec(memory_space=pl.ANY)] * len(args),
        out_specs=[pl.BlockSpec(memory_space=pltpu.VMEM)] * 2,
        scratch_shapes=[
            vm(coh.shape, coh.dtype), vm(vis.shape, F32), vm(gains.shape, F32), vm(wide.shape[1:], F32),
            vm(basis.shape[1:], F32), vm(coh_split, BF16), vm(vis_split, jnp.int16),
            vm(coh_split, BF16), vm(vis_split, jnp.int16), vm(gains_split, F32), vm((n,) + pairs.shape, jnp.int32),
            vm((2, n, LO, per), BF16), vm((hi * 2 * rows, LO), BF16), vm((hi * 3 * rows, LO), F32),
            vm((n,) + chunk, F32), vm((n - 1,) + chunk, F32), vm(chunk, F32),
            vm((m - 1,) + chunk, F32), vm(chunk, F32), vm((n,) + chunk, F32),
            vm((n,) + chunk, F32), vm(gains_split, F32), vm((n,) + chunk, F32), vm(gains_split, F32),
            vm(chunk, F32), vm((m - 1,) + chunk, F32),
            dma((5,)), dma((4, n - 1)), dma((4, n - 1)), dma((4,)),
            dma((n - 1,)), dma((n - 1,)), dma((m - 1,)), dma((m - 1,)), dma((n - 1,)), dma((n - 1,)),
            dma((2, n - 1)), dma((2, n - 1)), dma((m - 1,)), dma((m - 1,)),
        ],
        compiler_params=pltpu.CompilerParams(collective_id=0, has_side_effects=True, vmem_limit_bytes=VMEM_CAP),
    )(*args)


def shards(n, m, vis, coherency, gains_init, station_pairs):
    dirs = SKY_DIRECTIONS
    channels = vis.shape[1]
    per = vis.shape[2]
    owned = gains_init.shape[3]
    cl = channels // n
    rows = dirs * cl
    rho = 2.0 * per * n / STATION_TOTAL
    basis = basis_rows(channels * m)
    wide = np.zeros((m * n, 2, JD, dirs, 2, dirs, cl), np.float32)
    split = basis.reshape(JD, m * n, cl)
    for a in range(2):
        for d in range(dirs):
            wide[:, a, :, d, a, d, :] = np.moveaxis(split, 1, 0)
    wide = jnp.asarray(wide.reshape(m * n, JD * 2 * dirs, 2 * rows))
    basis_t = jnp.asarray(np.ascontiguousarray(basis.reshape(JD, m, channels).transpose(1, 2, 0)))

    args = (coherency, vis, gains_init, station_pairs, wide, basis_t)
    return tuple(calibrate(n, m, cl, rho, args, gains_init.shape))


def solution(mesh):
    placed = (
        P(None, "freq", "bl"),
        P(None, None, "freq", "bl"),
        P(None, None, "freq", "bl"),
        P(None, "bl"),
    )
    return jax.shard_map(
        functools.partial(shards, mesh.shape["bl"], mesh.shape["freq"]),
        mesh=mesh,
        in_specs=placed,
        out_specs=(P(None, None, "freq", "bl"), P(None, None, "freq", "bl")),
        check_vma=False,
    )
```

```python
import functools

import numpy as np
import jax
import jax.numpy as jnp
from jax import lax
from jax.experimental import pallas as pl
from jax.experimental.pallas import tpu as pltpu
from jax.sharding import PartitionSpec as P

STATION_TOTAL = 512
SKY_DIRECTIONS = 4
ITERS = 2
ROUNDS = 2
JD = 4
MESH = pl.DeviceIdType.MESH
HIGH = lax.Precision.HIGHEST
F32 = jnp.float32
BF16 = jnp.bfloat16
LO = 128
LO_SUM = 256
VIS_TOP = 60.0
VIS_STEPS = 32767.0
VMEM_CAP = 60 * 1024 * 1024


def basis_rows(channels):
    position = (2.0 * np.arange(channels, dtype=np.float32) + np.float32(1.0)) / np.float32(channels) - np.float32(1.0)
    raw = [np.ones_like(position), position, position * position, position * position * position]
    rows = []
    for vector in raw:
        for other in rows:
            vector = vector - np.sum(other * vector, dtype=np.float32) * other
        rows.append(vector / np.sqrt(np.sum(vector * vector, dtype=np.float32)))
    return np.stack(rows).astype(np.float32)


def greet(axes):
    barrier = pltpu.get_barrier_semaphore()
    for axis in axes:
        n = lax.axis_size(axis)
        me = lax.axis_index(axis)
        for o in range(1, n):
            pl.semaphore_signal(barrier, inc=1, device_id={axis: lax.rem(me + o, n)}, device_id_type=MESH)


def meet(axes):
    count = sum(lax.axis_size(axis) - 1 for axis in axes)
    pl.semaphore_wait(pltpu.get_barrier_semaphore(), count)


def sum_directions(x, cl):
    rows = x.shape[0]
    dirs = rows // cl
    if cl == 4 and rows == 16:
        half = x[:8] + x[8:]
        half = half + pltpu.roll(half, 4, 0)
        return jnp.concatenate([half, half], axis=0)
    total = x[:cl]
    for d in range(1, dirs):
        total = total + x[d * cl : (d + 1) * cl]
    return jnp.concatenate([total] * dirs, axis=0)


def flip(me, o, n):
    value = 0
    bit = 1
    while bit < n:
        value = value + lax.rem(lax.rem(lax.div(me, bit), 2) + lax.rem(lax.div(o, bit), 2), 2) * bit
        bit *= 2
    return value


def calibrate_kernel(
    n, m, cl, rho,
    coh_raw, vis_raw, gains_raw, pairs_in, wide_raw, basis_raw,
    gains_ref, cons_ref,
    coh_own, vis_own, gains_own, wide_ref, basis_ref, coh_send, vis_send,
    coh_all, vis_all, gains_all, pairs_all, onehot, upright, table, held, acc,
    part, got, chunk, got_f, whole, coef, fit_out, gains_send, got_b, got_g, chunk_b, got_fb,
    lr, sx, rx, lx, s1, r1, s2, r2, s3, r3, s4, r4, s5, r5,
):
    dirs = SKY_DIRECTIONS
    rows = dirs * cl
    lo = LO
    hi = STATION_TOTAL // lo
    per = vis_raw.shape[2]
    los = acc.shape[1]
    his = STATION_TOTAL // los
    owned = STATION_TOTAL // n
    me = lax.axis_index("bl")
    me_f = lax.axis_index("freq")
    greet(("bl", "freq"))
    loads = [
        pltpu.make_async_copy(gains_raw, gains_own, lr.at[0]),
        pltpu.make_async_copy(coh_raw, coh_own, lr.at[1]),
        pltpu.make_async_copy(vis_raw, vis_own, lr.at[2]),
        pltpu.make_async_copy(wide_raw.at[me_f * n + me], wide_ref, lr.at[3]),
        pltpu.make_async_copy(basis_raw.at[me_f], basis_ref, lr.at[4]),
    ]
    for copy in loads:
        copy.start()

    def transfer(a, o, peer, src, slot):
        ref = (gains_send, pairs_in, coh_send, vis_send)[a]
        dst = (gains_all, pairs_all, coh_all, vis_all)[a]
        return pltpu.make_async_remote_copy(
            ref if a == 1 else ref.at[src], dst.at[slot], sx.at[a, o - 1], rx.at[a, o - 1],
            device_id={"bl": peer}, device_id_type=MESH,
        )

    def of(x, s):
        return x[s * cl : (s + 1) * cl]

    loads[0].wait()
    parts = [[gains_own[a, d] for d in range(dirs)] for a in range(2)]
    for s in range(n):
        gains_send[s] = jnp.concatenate(
            [jnp.concatenate([of(x, s) for x in parts[a]], axis=0) for a in range(2)], axis=1
        )
    loads[1].wait()
    for a in range(2):
        parts = [coh_own[a, d].astype(F32) for d in range(dirs)]
        for s in range(n):
            coh_send[s, a] = jnp.concatenate([of(x, s) for x in parts], axis=0).astype(BF16)
    loads[2].wait()
    parts = [jnp.round(vis_own[a] * (VIS_STEPS / VIS_TOP)).astype(jnp.int32) for a in range(2)]
    for s in range(n):
        vis_send[s] = jnp.concatenate([of(x, s) for x in parts], axis=0).astype(jnp.int16)
    for copy in loads[3:]:
        copy.wait()
    meet(("bl", "freq"))

    sends = []
    for group in ((0, 1), (2, 3)):
        for o in range(1, n):
            peer = flip(me, o, n)
            for a in group:
                copy = transfer(a, o, peer, peer, me)
                copy.start()
                sends.append(copy)
    own = [
        pltpu.make_async_copy(gains_send.at[me], gains_all.at[me], lx.at[0]),
        pltpu.make_async_copy(pairs_in, pairs_all.at[me], lx.at[1]),
        pltpu.make_async_copy(coh_send.at[me], coh_all.at[me], lx.at[2]),
        pltpu.make_async_copy(vis_send.at[me], vis_all.at[me], lx.at[3]),
    ]
    for copy in own:
        copy.start()
    for copy in own:
        copy.wait()
    for o in range(1, n):
        transfer(0, o, flip(me, o, n), me, flip(me, o, n)).wait_recv()

    wide = wide_ref[...]

    def build(block):
        station = lax.broadcasted_iota(jnp.int32, (lo, per), 0)
        for t in range(2):
            index = pairs_all[block, t : t + 1, :] & (lo - 1)
            onehot[t, block] = jnp.where(station == index, 1.0, 0.0).astype(BF16)
            if los == lo:
                continue
            lanes = lax.broadcasted_iota(jnp.int32, (lo, los), 1)
            for p in range(per // lo):
                row = pairs_all[block, t : t + 1, p * lo : (p + 1) * lo] & (los - 1)
                column = jnp.transpose(jnp.broadcast_to(row, (lo, lo)))
                column = jnp.concatenate([column] * (los // lo), axis=1)
                upright[t, block, p * lo : (p + 1) * lo] = jnp.where(lanes == column, 1.0, 0.0).astype(BF16)

    def pick(x, group):
        value = x[: 2 * rows]
        for h in range(1, hi):
            value = jnp.where(group == h, x[2 * rows * h : 2 * rows * (h + 1)], value)
        return value

    def looked_up(block, t, at):
        row = pairs_all[block, t : t + 1, at : at + lo]
        index = jnp.broadcast_to(row & (lo - 1), (8, lo))
        group = jnp.broadcast_to(lax.shift_right_logical(row, lo.bit_length() - 1), (8, lo))
        out = []
        for r in range(0, 2 * rows, 8):
            value = None
            for h in range(hi):
                found = jnp.take_along_axis(held[h, r : r + 8], index, axis=1, mode="promise_in_bounds")
                value = found if value is None else jnp.where(group == h, found, value)
            out.append(value)
        return jnp.concatenate(out, axis=0)

    def gather(block, t, group, tiles):
        parts = [looked_up(block, t, p * lo) for p in range(tiles)]
        if tiles * lo < per:
            ahead = tiles * lo
            parts.append(
                pick(
                    jnp.dot(table[...], onehot[t, block, :, ahead:], preferred_element_type=F32), group[:, ahead:]
                )
            )
        return jnp.concatenate(parts, axis=1)

    def spread(terms, group):
        terms = jnp.concatenate(terms, axis=0).astype(BF16)
        return jnp.concatenate(
            [
                terms * jnp.broadcast_to(jnp.where(group == h, 1.0, 0.0), terms.shape).astype(BF16)
                for h in range(his)
            ],
            axis=0,
        )

    def sums_of(block):
        group0 = lax.shift_right_logical(pairs_all[block, 0:1, :], lo.bit_length() - 1)
        group1 = lax.shift_right_logical(pairs_all[block, 1:2, :], lo.bit_length() - 1)
        ohn = onehot[0, block]
        ohf = onehot[1, block]
        near = gather(block, 0, group0, min(16, per // lo))
        far = gather(block, 1, group1, min(0, per // lo))
        nr, ni = near[:rows], near[rows:]
        fr, fi = far[:rows], far[rows:]
        cr = coh_all[block, 0].astype(F32)
        ci = coh_all[block, 1].astype(F32)
        zr = cr * fr + ci * fi
        zi = ci * fr - cr * fi
        xr = nr * cr - ni * ci
        xi = nr * ci + ni * cr
        mr = sum_directions(nr * zr - ni * zi, cl)
        mi = sum_directions(nr * zi + ni * zr, cl)
        v = vis_all[block].astype(jnp.int32).astype(F32) * (VIS_TOP / VIS_STEPS)
        rr = jnp.concatenate([v[:cl]] * dirs, axis=0) - mr
        ri = jnp.concatenate([v[cl:]] * dirs, axis=0) - mi
        t1 = spread([rr * zr + ri * zi, ri * zr - rr * zi, zr * zr + zi * zi], lax.shift_right_logical(pairs_all[block, 0:1, :], los.bit_length() - 1))
        t2 = spread([rr * xr + ri * xi, rr * xi - ri * xr, xr * xr + xi * xi], lax.shift_right_logical(pairs_all[block, 1:2, :], los.bit_length() - 1))
        if los > lo:
            return jnp.dot(t1, upright[0, block], preferred_element_type=F32) + jnp.dot(
                t2, upright[1, block], preferred_element_type=F32
            )
        contract = (((1,), (1,)), ((), ()))
        return lax.dot_general(t1, ohn, contract, preferred_element_type=F32) + lax.dot_general(
            t2, ohf, contract, preferred_element_type=F32
        )

    def add_block(block):
        acc[...] += sums_of(block)

    def load_table(gains):
        rounded = gains.astype(BF16)
        for h in range(hi):
            held[h] = rounded[:, h * lo : (h + 1) * lo].astype(F32)
        table[...] = jnp.concatenate([rounded[:, h * lo : (h + 1) * lo] for h in range(hi)], axis=0)
        acc[...] = jnp.zeros_like(acc)

    def advance(gains, target):
        sums = jnp.concatenate([acc[3 * rows * h : 3 * rows * (h + 1)] for h in range(his)], axis=1)
        below = 2.0 * sums[2 * rows :] + rho
        below = jnp.concatenate([below, below], axis=0)
        return gains + (sums[: 2 * rows] + rho * (target - gains)) / below

    def again(block, carry):
        acc[...] += sums_of(2 * block) + sums_of(2 * block + 1)
        return carry

    def whole_rows(ref):
        blocks = [ref[s] for s in range(n)]
        return jnp.concatenate(
            [jnp.concatenate([b[:, a * owned : (a + 1) * owned] for b in blocks], axis=1) for a in range(2)], axis=0
        )

    def block_of(x, s):
        half = x.shape[0] // 2
        return jnp.concatenate([x[:half, s * owned : (s + 1) * owned], x[half:, s * owned : (s + 1) * owned]], axis=1)

    def start_freq(src, slots, send, recv):
        copies = []
        for o in range(1, m):
            copy = pltpu.make_async_remote_copy(
                src, slots.at[o - 1], send.at[o - 1], recv.at[o - 1],
                device_id={"freq": lax.rem(me_f + o, m)}, device_id_type=MESH,
            )
            copy.start()
            copies.append(copy)
        return copies

    def sum_freq(copies, total, slots):
        for o in range(1, m):
            copies[o - 1].wait()
            total = total + slots[o - 1]
        return total

    gains = whole_rows(gains_all)
    target = gains
    load_table(gains)

    def arriving(o, carry):
        peer = flip(me, o, n)
        for a in (2, 3):
            transfer(a, o, peer, me, peer).wait_recv()
        add_block(peer)
        return carry

    def known(o, carry):
        peer = flip(me, o, n)
        transfer(1, o, peer, me, peer).wait_recv()
        build(peer)
        return carry

    build(me)
    add_block(me)
    lax.fori_loop(1, n, known, 0)
    lax.fori_loop(1, n, arriving, 0)
    gains = advance(gains, target)
    for _ in range(ITERS - 1):
        load_table(gains)
        lax.fori_loop(0, n // 2, again, 0)
        gains = advance(gains, target)
    for copy in sends:
        copy.wait_send()

    fitted = jnp.dot(wide, gains, precision=HIGH, preferred_element_type=F32)
    for s in range(n):
        part[s] = block_of(fitted, s)
    copies = []
    for o in range(1, n):
        peer = flip(me, o, n)
        copy = pltpu.make_async_remote_copy(
            part.at[peer], got.at[o - 1], s1.at[o - 1], r1.at[o - 1],
            device_id={"bl": peer}, device_id_type=MESH,
        )
        copy.start()
        copies.append(copy)
    load_table(gains)
    cut = (n // 8, n * 3 // 8)
    lax.fori_loop(0, cut[0], again, 0)
    total = part[me]
    for o in range(1, n):
        copies[o - 1].wait()
        total = total + got[o - 1]
    chunk[...] = total
    copies = start_freq(chunk, got_f, s2, r2)
    lax.fori_loop(cut[0], cut[1], again, 0)
    total = sum_freq(copies, total, got_f)
    whole[...] = total
    copies = []
    for o in range(1, n):
        copy = pltpu.make_async_remote_copy(
            whole, coef.at[me], s3.at[o - 1], r3.at[o - 1],
            device_id={"bl": flip(me, o, n)}, device_id_type=MESH,
        )
        copy.start()
        copies.append(copy)
    coef[me] = total
    lax.fori_loop(cut[1], n // 2, again, 0)
    for copy in copies:
        copy.wait_send()
    for o in range(1, n):
        peer = flip(me, o, n)
        pltpu.make_async_remote_copy(
            whole, coef.at[peer], s3.at[o - 1], r3.at[o - 1],
            device_id={"bl": peer}, device_id_type=MESH,
        ).wait_recv()

    consensus = lax.dot_general(
        wide, whole_rows(coef), (((0,), (0,)), ((), ())), precision=HIGH, preferred_element_type=F32
    )
    dual = gains - consensus
    target = consensus - dual
    gains = advance(gains, target)
    for _ in range(ITERS - 1):
        load_table(gains)
        lax.fori_loop(0, n // 2, again, 0)
        gains = advance(gains, target)

    fitted = jnp.dot(wide, gains + dual, precision=HIGH, preferred_element_type=F32)
    for s in range(n):
        fit_out[s] = block_of(fitted, s)
        gains_send[s] = block_of(gains, s)

    def deliver(k, o, peer, slot):
        src, dst = ((fit_out, got_b), (gains_send, got_g))[k]
        return pltpu.make_async_remote_copy(
            src.at[peer], dst.at[slot], s4.at[k, o - 1], r4.at[k, o - 1],
            device_id={"bl": peer}, device_id_type=MESH,
        )

    copies = []
    for k in range(2):
        for o in range(1, n):
            copy = deliver(k, o, flip(me, o, n), me)
            copy.start()
            copies.append(copy)
    got_b[me] = fit_out[me]
    got_g[me] = gains_send[me]
    for o in range(1, n):
        deliver(0, o, flip(me, o, n), flip(me, o, n)).wait_recv()
    total = got_b[0]
    for s in range(1, n):
        total = total + got_b[s]
    chunk_b[...] = total
    total = sum_freq(start_freq(chunk_b, got_fb, s5, r5), total, got_fb)
    for o in range(1, n):
        deliver(1, o, flip(me, o, n), flip(me, o, n)).wait_recv()
    for copy in copies:
        copy.wait_send()
    for s in range(n):
        for a in range(2):
            for d in range(dirs):
                gains_ref[a, d, s * cl : (s + 1) * cl, :] = got_g[s, d * cl : (d + 1) * cl, a * owned : (a + 1) * owned]
    mine = basis_ref[...]
    for a in range(2):
        for d in range(dirs):
            value = None
            for j in range(JD):
                row = j * dirs + d
                term = mine[:, j : j + 1] * total[row : row + 1, a * owned : (a + 1) * owned]
                value = term if value is None else value + term
            cons_ref[a, d] = value


def calibrate(n, m, cl, rho, args, shape):
    coh, vis, gains, pairs, wide, basis = args
    rows = SKY_DIRECTIONS * cl
    hi = STATION_TOTAL // LO
    per = vis.shape[2]
    owned = STATION_TOTAL // n
    los = LO_SUM if n * per <= 16384 else LO
    tall = (2, n, per, los) if los > LO else (8, LO)
    coh_split = (n, 2, rows, per)
    vis_split = (n, 2 * cl, per)
    gains_split = (n, rows, 2 * owned)
    chunk = (JD * SKY_DIRECTIONS, 2 * owned)
    dma = pltpu.SemaphoreType.DMA
    vm = pltpu.VMEM
    return pl.pallas_call(
        functools.partial(calibrate_kernel, n, m, cl, rho),
        out_shape=[jax.ShapeDtypeStruct(shape, F32)] * 2,
        in_specs=[pl.BlockSpec(memory_space=pl.ANY)] * len(args),
        out_specs=[pl.BlockSpec(memory_space=pltpu.VMEM)] * 2,
        scratch_shapes=[
            vm(coh.shape, coh.dtype), vm(vis.shape, F32), vm(gains.shape, F32), vm(wide.shape[1:], F32),
            vm(basis.shape[1:], F32), vm(coh_split, BF16), vm(vis_split, jnp.int16),
            vm(coh_split, BF16), vm(vis_split, jnp.int16), vm(gains_split, F32), vm((n,) + pairs.shape, jnp.int32),
            vm((2, n, LO, per), BF16), vm(tall, BF16), vm((hi * 2 * rows, LO), BF16),
            vm((hi, 2 * rows, LO), F32), vm((STATION_TOTAL // los * 3 * rows, los), F32),
            vm((n,) + chunk, F32), vm((n - 1,) + chunk, F32), vm(chunk, F32),
            vm((m - 1,) + chunk, F32), vm(chunk, F32), vm((n,) + chunk, F32),
            vm((n,) + chunk, F32), vm(gains_split, F32), vm((n,) + chunk, F32), vm(gains_split, F32),
            vm(chunk, F32), vm((m - 1,) + chunk, F32),
            dma((5,)), dma((4, n - 1)), dma((4, n - 1)), dma((4,)),
            dma((n - 1,)), dma((n - 1,)), dma((m - 1,)), dma((m - 1,)), dma((n - 1,)), dma((n - 1,)),
            dma((2, n - 1)), dma((2, n - 1)), dma((m - 1,)), dma((m - 1,)),
        ],
        compiler_params=pltpu.CompilerParams(collective_id=0, has_side_effects=True, vmem_limit_bytes=VMEM_CAP),
    )(*args)


def shards(n, m, vis, coherency, gains_init, station_pairs):
    dirs = SKY_DIRECTIONS
    channels = vis.shape[1]
    per = vis.shape[2]
    owned = gains_init.shape[3]
    cl = channels // n
    rows = dirs * cl
    rho = 2.0 * per * n / STATION_TOTAL
    basis = basis_rows(channels * m)
    wide = np.zeros((m * n, 2, JD, dirs, 2, dirs, cl), np.float32)
    split = basis.reshape(JD, m * n, cl)
    for a in range(2):
        for d in range(dirs):
            wide[:, a, :, d, a, d, :] = np.moveaxis(split, 1, 0)
    wide = jnp.asarray(wide.reshape(m * n, JD * 2 * dirs, 2 * rows))
    basis_t = jnp.asarray(np.ascontiguousarray(basis.reshape(JD, m, channels).transpose(1, 2, 0)))

    args = (coherency, vis, gains_init, station_pairs, wide, basis_t)
    return tuple(calibrate(n, m, cl, rho, args, gains_init.shape))


def solution(mesh):
    placed = (
        P(None, "freq", "bl"),
        P(None, None, "freq", "bl"),
        P(None, None, "freq", "bl"),
        P(None, "bl"),
    )
    return jax.shard_map(
        functools.partial(shards, mesh.shape["bl"], mesh.shape["freq"]),
        mesh=mesh,
        in_specs=placed,
        out_specs=(P(None, None, "freq", "bl"), P(None, None, "freq", "bl")),
        check_vma=False,
    )
```
